32 devices in a mesh: chan: 16 (over z, y, x), blk: 2 (over core).
Axes of the slice: x: 2, y: 2, z: 4, core: 2. Of those that a mesh axis runs over, the one named last changes fastest.
Arguments:
- generator: bfloat16 [16, 1536, 1536], P('chan', 'blk'), may hold values from -6 to 6
- hamiltonian: bfloat16 [16, 1536, 1536], P('chan', 'blk'), may hold values from -0.15625 to 0.15625
- pp_occupancy: float32 [16, 1536], P('chan'), may hold values from -1 to 1
- ph_occupancy: float32 [16, 1536], P('chan'), may hold values from -1 to 1
- lengths: int32 [16], P('chan'), may hold values from 384 to 1536, as said below
- partner: int32 [16, 16], P('chan'), may hold values from 0 to 15, each once within a row
- coupling: float32 [16, 16], P('chan'), may hold values from 0.5 to 2
- degeneracy: float32 [16], P('chan'), may hold values from 1 to 30
- orbital: int32 [16, 1536], P('chan', 'blk'), may hold values from 0 to 239
Outputs:
- two_body: bfloat16 [16, 1536, 1536], P('chan', 'blk')
- one_body: float32 [240], replicated
The draws below stay inside these ranges and needn't reach their ends.
Inputs may be any that keep to these rules, and one draw needn't show every extreme that they name: `lengths`: some channel has the full length 1536.
All inputs are finite; a program needn't handle non-finite values.
Results may differ from the reference program's by a relative error of at most 0.007.
Values may be sent and summed in bfloat16 or wider, within the bound.
A program may use at most 128 MiB of HBM per device.

```python
import math
import jax
import jax.numpy as jnp
from jax import lax

M = 1536
NOB = 240
NCH = 16
PIECE = 48
N_CHAN = 16
N_BLK = 2


def draw_lengths(key, part):
    first_key, second_key = jax.random.split(jax.random.fold_in(key, 11))
    sizes = jax.random.randint(first_key, (NCH,), M // 4, M + 1, dtype=jnp.int32)
    chosen = jax.random.randint(second_key, (), 0, NCH, dtype=jnp.int32)
    return jnp.where(jnp.arange(NCH, dtype=jnp.int32) == chosen, M, sizes).astype(jnp.int32)


def touch_ends(entries, rng, least, largest):
    dims = entries.shape
    spot = [jax.random.randint(jax.random.fold_in(rng, axis), (), 0, dims[axis]) for axis in range(len(dims))]
    entries = entries.at[tuple(spot)].set(least)
    longest = dims.index(max(dims))
    spot[longest] = (spot[longest] + 1) % dims[longest]
    return entries.at[tuple(spot)].set(largest)


def steps_of(rng, shape, cuts, smallest, top_value):
    factor_of = 1.0
    for position, blocks in cuts:
        draws = jax.random.uniform(jax.random.fold_in(jax.random.fold_in(rng, 6), position), (blocks,), jnp.float32, smallest / len(cuts), top_value / len(cuts))
        factor_of = factor_of * jnp.repeat(jnp.exp(draws), shape[position] // blocks).reshape((-1,) + (1,) * (len(shape) - 1 - position))
    return factor_of


def bell_draw(key, shape, deviation, most, cuts=(), kind=jnp.bfloat16):
    entries = deviation * jax.random.normal(key, shape, jnp.float32)
    if cuts:
        entries = entries * steps_of(key, shape, cuts, -0.22, 0.18)
    return jnp.clip(entries, -most, most).astype(kind)


def setup_inputs(seed: int = 0) -> dict:
    seeds = jax.random.split(jax.random.key(seed), 10)
    return {
        "generator": bell_draw(seeds[0], (NCH, M, M), 1.0, 6.0, ((0, 16), (1, 2))),
        "hamiltonian": bell_draw(seeds[1], (NCH, M, M), M ** -0.5, 0.15625, ((0, 16), (1, 2))),
        "pp_occupancy": jnp.clip(jax.random.uniform(seeds[2], (NCH, M), jnp.float32, -1.0, 1.0) * steps_of(seeds[2], (NCH, M), ((0, 16),), -0.4, 0.0), -1.0, 1.0),
        "ph_occupancy": jnp.clip(jax.random.uniform(seeds[3], (NCH, M), jnp.float32, -1.0, 1.0) * steps_of(seeds[3], (NCH, M), ((0, 16),), -0.4, 0.0), -1.0, 1.0),
        "lengths": draw_lengths(jax.random.fold_in(seeds[9], 71), 0),
        "partner": jax.vmap(lambda own: jax.random.permutation(own, N_CHAN))(jax.random.split(seeds[5], NCH)).reshape((NCH, N_CHAN)).astype(jnp.int32),
        "coupling": jnp.clip(jnp.exp(math.log(2.0) - 1.3862944 * jax.random.uniform(seeds[6], (NCH, N_CHAN), jnp.float32) ** steps_of(seeds[6], (NCH, N_CHAN), ((0, 16),), -0.2, 0.2)), 0.5, 2.0),
        "degeneracy": jnp.clip(jnp.exp(math.log(30.0) - 3.4011974 * jax.random.uniform(seeds[7], (NCH,), jnp.float32) ** steps_of(seeds[7], (NCH,), ((0, 16),), -0.2, 0.2)), 1.0, 30.0),
        "orbital": touch_ends(jax.random.randint(seeds[8], (NCH, M), 0, NOB), jax.random.fold_in(seeds[8], 1), 0, NOB - 1).astype(jnp.int32),
    }


def commute(first_mat, second_mat, occupancy):
    left = (first_mat.astype(jnp.float32) * occupancy[None, :]).astype(jnp.bfloat16)
    right = (second_mat.astype(jnp.float32) * occupancy[None, :]).astype(jnp.bfloat16)
    return jnp.dot(left, second_mat, preferred_element_type=jnp.float32) - jnp.dot(right, first_mat, preferred_element_type=jnp.float32)

def commute_items(items):
    return commute(items[0], items[1], items[2])

def recouple(matrices, partner, coupling):
    layout = (NCH, N_BLK, N_CHAN, PIECE, M)
    pieces = matrices.reshape(layout)
    scaled = (pieces.astype(jnp.float32) * coupling[:, None, :, None, None]).astype(jnp.bfloat16)
    sender_slot = jnp.argsort(partner, axis=1).astype(jnp.int32)
    moved = jnp.take_along_axis(scaled, sender_slot[:, None, :, None, None], axis=2)
    return jnp.transpose(moved, (2, 1, 0, 3, 4)).reshape(NCH, M, M)

def reference(generator, hamiltonian, pp_occupancy, ph_occupancy, lengths, partner, coupling, degeneracy, orbital):
    positions = jnp.arange(M, dtype=jnp.int32)
    live_cols = positions[None, :] < lengths[:, None]
    live_mask = live_cols[:, :, None] & live_cols[:, None, :]
    gen_live = jnp.where(live_mask, generator, jnp.zeros((), generator.dtype))
    ham_live = jnp.where(live_mask, hamiltonian, jnp.zeros((), hamiltonian.dtype))
    ladder = lax.map(commute_items, (gen_live, ham_live, pp_occupancy))
    gen_cross = recouple(gen_live, partner, coupling)
    ham_cross = recouple(ham_live, partner, coupling)
    crossed = lax.map(commute_items, (gen_cross, ham_cross, ph_occupancy)).astype(jnp.bfloat16)
    layout = (NCH, N_BLK, N_CHAN, PIECE, M)
    turned = jnp.transpose(crossed.reshape(layout), (2, 1, 0, 3, 4))
    fetched = jnp.take_along_axis(turned, partner.astype(jnp.int32)[:, None, :, None, None], axis=2)
    restored = (fetched.astype(jnp.float32) * coupling[:, None, :, None, None]).reshape(NCH, M, M)
    combined = jnp.where(live_mask, ladder + restored, jnp.zeros((), jnp.float32))
    two_body = combined.astype(jnp.bfloat16)
    diagonal = jnp.diagonal(combined, axis1=1, axis2=2) * degeneracy[:, None]
    summed = jax.ops.segment_sum(diagonal.reshape(-1), orbital.reshape(-1).astype(jnp.int32), num_segments=NOB)
    one_body = summed / (8.0 * math.sqrt(NCH * M / NOB))
    return (two_body, one_body)
```

```python
import functools
import math

import jax
import jax.numpy as jnp
from jax import lax
from jax.experimental import pallas as pl
from jax.experimental.pallas import tpu as pltpu
from jax.sharding import PartitionSpec as P

NOB = 240
MESH = pl.DeviceIdType.MESH
VMEM_LIMIT = 60 * 1024 * 1024


def scaled_copy(matrix, occupancy):
    return (matrix.astype(jnp.float32) * occupancy[None, :]).astype(jnp.bfloat16)


def make_fold(left_scaled, right_scaled, pieces):
    return jnp.dot(left_scaled, pieces[1], preferred_element_type=jnp.float32) - jnp.dot(
        right_scaled, pieces[0], preferred_element_type=jnp.float32
    )


def on_device_plain(
    generator,
    hamiltonian,
    pp_occupancy,
    ph_occupancy,
    lengths,
    partner,
    coupling,
    degeneracy,
    orbital,
):
    chan_count = lax.axis_size("chan")
    blk_index = lax.axis_index("blk")
    row_count = generator.shape[1]
    columns = generator.shape[2]
    piece_rows = row_count // chan_count
    col_ids = jnp.arange(columns, dtype=jnp.int32)
    row_ids = blk_index * row_count + jnp.arange(row_count, dtype=jnp.int32)
    live_mask = (row_ids[:, None] < lengths[0]) & (col_ids[None, :] < lengths[0])
    nothing = jnp.zeros((), jnp.bfloat16)
    gen_live = jnp.where(live_mask, generator[0], nothing)
    ham_live = jnp.where(live_mask, hamiltonian[0], nothing)
    gen_scaled = scaled_copy(gen_live, pp_occupancy[0])
    ham_scaled = scaled_copy(ham_live, pp_occupancy[0])
    owner_ids = jnp.arange(chan_count, dtype=jnp.int32)
    matches = partner[0][None, :] == owner_ids[:, None]
    sender_slot = jnp.sum(jnp.where(matches, owner_ids[None, :], 0), axis=1)
    scales = coupling[0]
    scales_slot = scales[sender_slot]
    ph_occ = ph_occupancy[0]
    gen_send = (
        gen_live.reshape(chan_count, piece_rows, columns)[sender_slot].astype(jnp.float32)
        * scales_slot[:, None, None]
    ).astype(jnp.bfloat16)
    ham_send = (
        ham_live.reshape(chan_count, piece_rows, columns)[sender_slot].astype(jnp.float32)
        * scales_slot[:, None, None]
    ).astype(jnp.bfloat16)
    gen_recv, ham_recv = (
        lax.all_to_all(gen_send, "chan", split_axis=0, concat_axis=0, tiled=True),
        lax.all_to_all(ham_send, "chan", split_axis=0, concat_axis=0, tiled=True),
    )
    ladder = make_fold(
        gen_scaled,
        ham_scaled,
        (
            lax.all_gather(gen_live, "blk", axis=0, tiled=True),
            lax.all_gather(ham_live, "blk", axis=0, tiled=True),
        ),
    )
    gen_rows = gen_recv.reshape(row_count, columns)
    ham_rows = ham_recv.reshape(row_count, columns)
    crossed = make_fold(
        scaled_copy(gen_rows, ph_occ),
        scaled_copy(ham_rows, ph_occ),
        (
            lax.all_gather(gen_rows, "blk", axis=0, tiled=True),
            lax.all_gather(ham_rows, "blk", axis=0, tiled=True),
        ),
    )
    crossed_back = crossed.astype(jnp.bfloat16).reshape(chan_count, piece_rows, columns)
    returned = lax.all_to_all(crossed_back, "chan", split_axis=0, concat_axis=0, tiled=True)
    restored = (returned[partner[0]].astype(jnp.float32) * scales[:, None, None]).reshape(
        row_count, columns
    )
    combined = jnp.where(live_mask, ladder + restored, jnp.zeros((), jnp.float32))
    two_body = combined.astype(jnp.bfloat16)[None]
    own_block = lax.dynamic_slice_in_dim(combined, blk_index * row_count, row_count, 1)
    weighted = jnp.diagonal(own_block) * degeneracy[0]
    orbit_match = orbital[0][:, None] == jnp.arange(NOB, dtype=jnp.int32)[None, :]
    partial_sums = jnp.sum(jnp.where(orbit_match, weighted[:, None], 0.0), axis=0)
    normalizer = 8.0 * math.sqrt(chan_count * columns / NOB)
    one_body = lax.psum(partial_sums, ("chan", "blk")) / normalizer
    return (two_body, one_body)


def widths_of(columns):
    unit = 256
    inner = columns - 2 * unit
    if inner <= 0 or inner % (2 * unit):
        return (unit,) * (columns // unit)
    return (unit,) + (2 * unit,) * (inner // (2 * unit)) + (unit,)


def fused_kernel(n, m, widths, scale, *refs):
    parts = len(widths)
    (
        gen_hbm,
        ham_hbm,
        pp_ref,
        ph_ref,
        partner_ref,
        coupling_ref,
        length_ref,
        weight_ref,
        orbital_ref,
        out_hbm,
        sum_ref,
        own_g,
        own_h,
        far_g,
        far_h,
        send_g,
        send_h,
        cross_g,
        cross_h,
        left,
        right,
        lad,
        out,
        diag,
        part,
        slots,
    ) = refs[:26]
    back = refs[26 : 26 + parts]
    ret = refs[26 + parts : 26 + 2 * parts]
    (
        own_sem,
        x_send,
        x_recv,
        a_send,
        a_recv,
        r_send,
        r_recv,
        l_sem,
        b_send,
        b_recv,
        out_sem,
        t_send,
        t_recv,
    ) = refs[26 + 2 * parts :]
    c = lax.axis_index("chan")
    b = lax.axis_index("blk")
    ob = 1 - b
    me = c * m + b
    count = n * m
    piece, columns = gen_hbm.shape[1:]
    rows = n * piece
    orbits = part.shape[1]
    twin = (c, ob)
    ends = [sum(widths[: j + 1]) for j in range(parts)]
    starts = [
        pl.multiple_of((1 - b) * (ends[j] - widths[j]) + b * (columns - ends[j]), 128)
        for j in range(parts)
    ]
    middle = [end >= rows for end in ends].index(True)
    raw = ((gen_hbm, own_g, far_g), (ham_hbm, own_h, far_h))
    sent = ((send_g, cross_g), (send_h, cross_h))
    length = length_ref[0]

    def half_cols(half):
        return pl.ds(pl.multiple_of(half * rows, 128), rows)

    def slot(half, d):
        return pl.ds(pl.multiple_of((half * n + d) * piece, piece), piece)

    def strip(d):
        return pl.ds(pl.multiple_of(d * piece, piece), piece)

    level = n // 4
    z, y, x = c // level, c % level // 2, c % 2

    def chip(to, turn):
        return to * level + (y + turn // 2) % (level // 2) * 2 + (x + turn) % 2

    def pick(i, first, second, third):
        q, r = i // level, i % level
        own = q // 3
        to = first * ((1 - q) * (2 - q) // 2) + second * (q * (2 - q)) + third * (q * (q - 1) // 2)
        turn = r + b * (level - 1 - 2 * r)
        return chip(to * (1 - own) + z * own, turn * (1 - own) + (r + 1) * own)

    def target(i):
        return pick(i, 1 + z % 2, 3 * (1 - z % 2), (z + 2) % 4)

    def source(i):
        return pick(i, z + 1 - 2 * (z % 2), 2 - z // 2, 3 * (1 - z // 2))

    def each(count, body, first=0):
        def step(i, carry):
            body(i)
            return carry

        lax.fori_loop(first, count, step, 0)

    def own_copy(t):
        return pltpu.make_async_copy(raw[t][0], raw[t][1], own_sem.at[t])

    def twin_copy(t):
        return pltpu.make_async_remote_copy(
            src_ref=raw[t][0],
            dst_ref=raw[t][2],
            send_sem=x_send.at[t],
            recv_sem=x_recv.at[t],
            device_id=twin,
            device_id_type=MESH,
        )

    def piece_copy(t, k, d):
        return pltpu.make_async_remote_copy(
            src_ref=sent[t][0].at[strip(k)],
            dst_ref=sent[t][1].at[slot(b, d)],
            send_sem=a_send.at[t, k],
            recv_sem=a_recv.at[t, d],
            device_id=(k, b),
            device_id_type=MESH,
        )

    def relay(t, half, d):
        return pltpu.make_async_remote_copy(
            src_ref=sent[t][1].at[slot(half, d)],
            dst_ref=sent[t][1].at[slot(half, d)],
            send_sem=r_send.at[t, d],
            recv_sem=r_recv.at[t, d],
            device_id=twin,
            device_id_type=MESH,
        )

    def back_copy(j, k, d):
        return pltpu.make_async_remote_copy(
            src_ref=back[j].at[strip(k)],
            dst_ref=ret[j].at[d],
            send_sem=b_send.at[j, k],
            recv_sem=b_recv.at[j, d],
            device_id=(k, b),
            device_id_type=MESH,
        )

    def back_local(j):
        return pltpu.make_async_copy(back[j].at[strip(c)], ret[j].at[c], l_sem.at[j])

    def out_copy(j):
        cols = pl.ds(starts[j], widths[j])
        return pltpu.make_async_copy(out.at[:, cols], out_hbm.at[:, cols], out_sem.at[j])

    def peer(i):
        return (me + 1 + i) % count

    def total_copy(to, origin):
        return pltpu.make_async_remote_copy(
            src_ref=part,
            dst_ref=slots.at[origin],
            send_sem=t_send.at[to],
            recv_sem=t_recv.at[origin],
            device_id=(to // m, to % m),
            device_id_type=MESH,
        )

    for t in range(2):
        own_copy(t).start()
    barrier = pltpu.get_barrier_semaphore()

    def greet(i):
        to = peer(i)
        pl.semaphore_signal(barrier, inc=1, device_id=(to // m, to % m), device_id_type=MESH)

    each(count - 1, greet)
    for t in range(2):
        own_copy(t).wait()

    col_live = lax.broadcasted_iota(jnp.int32, (1, columns), 1) < length
    row_ids = lax.broadcasted_iota(jnp.int32, (piece, 1), 0)

    def prepare(k, refs_at):
        p, weight = jnp.int32(0), jnp.float32(0.0)
        for q in range(n):
            match = partner_ref[q] == k
            p = jnp.where(match, q, p)
            weight = jnp.where(match, coupling_ref[q], weight)
        factor = jnp.where(col_live, weight, 0.0)
        factor = jnp.where(row_ids + (b * n + p) * piece < length, factor, 0.0)
        for t in range(2):
            dst, where = refs_at[t]
            dst[where, :] = (raw[t][1][p].astype(jnp.float32) * factor).astype(jnp.bfloat16)

    def prepare_sent(i):
        k = target(i)
        prepare(k, [(send_g, strip(k)), (send_h, strip(k))])

    def send(i):
        k = target(i)
        for t in range(2):
            piece_copy(t, k, c).start()

    prepare_sent(0)
    pl.semaphore_wait(barrier, count - 1)
    distant = n - level

    def prepare_and_send(i):
        prepare_sent(i)
        send(i - 1)

    each(distant, prepare_and_send, 1)
    prepare(c, [(cross_g, slot(b, c)), (cross_h, slot(b, c))])
    send(distant - 1)
    for t in range(2):
        twin_copy(t).start()
    each(n - 1, prepare_sent, distant)

    def pp_scale(i):
        factor = jnp.where(col_live, pp_ref[...], 0.0)
        left[strip(i), :] = (own_g[i].astype(jnp.float32) * factor).astype(jnp.bfloat16)
        right[strip(i), :] = (own_h[i].astype(jnp.float32) * factor).astype(jnp.bfloat16)

    each(n, pp_scale)

    def dot(x, y):
        return jnp.dot(x, y, preferred_element_type=jnp.float32)

    for t in range(2):
        relay(t, b, c).start()
        twin_copy(t).wait_recv()
    unit = 256

    def ladder_step(j):
        cols = pl.ds(pl.multiple_of(j * unit, unit), unit)
        near, other = half_cols(b), half_cols(ob)
        lad[:, cols] = (
            dot(left[:, near], own_h[:, :, cols].reshape(rows, unit))
            + dot(left[:, other], far_h[:, :, cols].reshape(rows, unit))
            - dot(right[:, near], own_g[:, :, cols].reshape(rows, unit))
            - dot(right[:, other], far_g[:, :, cols].reshape(rows, unit))
        )

    each(columns // unit, ladder_step)
    each(n - 1, send, distant)

    def ph_scale(d):
        factor = ph_ref[...]
        left[strip(d), :] = (cross_g[slot(b, d), :].astype(jnp.float32) * factor).astype(jnp.bfloat16)
        right[strip(d), :] = (cross_h[slot(b, d), :].astype(jnp.float32) * factor).astype(jnp.bfloat16)

    ph_scale(c)

    def take(i):
        d = source(i)
        for t in range(2):
            piece_copy(t, d, d).wait_recv()
            relay(t, b, d).start()
        ph_scale(d)

    each(n - 1, take)

    def take_relay(d):
        for t in range(2):
            relay(t, ob, d).wait_recv()

    each(n, take_relay)

    for j in range(parts):
        cols = pl.ds(starts[j], widths[j])
        back[j][...] = (dot(left[...], cross_h[:, cols]) - dot(right[...], cross_g[:, cols])).astype(
            jnp.bfloat16
        )

        def give(i, j=j):
            back_copy(j, target(i), c).start()

        each(n - 1, give)
        back_local(j).start()

    first = b * rows
    for j in range(parts):

        def take_back(i, j=j):
            d = source(i)
            back_copy(j, d, d).wait_recv()

        each(n - 1, take_back)
        back_local(j).wait()
        cols = pl.ds(starts[j], widths[j])
        col_ids = starts[j] + lax.broadcasted_iota(jnp.int32, (1, widths[j]), 1)
        diag[:, cols] = jnp.zeros((1, widths[j]), jnp.float32)

        def fold(p, j=j, cols=cols, col_ids=col_ids):
            ids = row_ids + (first + p * piece)
            value = lad[strip(p), cols] + ret[j][partner_ref[p]].astype(jnp.float32) * coupling_ref[p]
            value = jnp.where((ids < length) & (col_ids < length), value, 0.0)
            out[strip(p), cols] = value.astype(jnp.bfloat16)
            diag[:, cols] += jnp.sum(jnp.where(ids == col_ids, value, 0.0), axis=0, keepdims=True)

        each(n, fold)
        out_copy(j).start()
        if j != middle:
            continue
        weighted = diag[:, half_cols(b)] * weight_ref[0]
        hits = lax.broadcasted_iota(jnp.int32, (orbits, rows), 0) == orbital_ref[...]
        part[...] = lax.dot_general(
            weighted,
            jnp.where(hits, 1.0, 0.0),
            (((1,), (1,)), ((), ())),
            precision=lax.Precision.HIGHEST,
            preferred_element_type=jnp.float32,
        )

        def total_send(i):
            total_copy(peer(i), me).start()

        each(count - 1, total_send)
        slots[me] = part[...]

    for t in range(2):
        twin_copy(t).wait_send()

    def drain(i):
        k = target(i)
        for t in range(2):
            piece_copy(t, k, c).wait_send()
        for j in range(parts):
            back_copy(j, k, c).wait_send()

    each(n - 1, drain)

    def drain_relay(d):
        for t in range(2):
            relay(t, b, d).wait_send()

    each(n, drain_relay)

    def total_take(i):
        other = peer(i)
        total_copy(other, me).wait_send()
        total_copy(other, other).wait_recv()

    each(count - 1, total_take)
    sum_ref[...] = jnp.sum(slots[...], axis=0) * scale
    for j in range(parts):
        out_copy(j).wait()


def on_device(
    generator,
    hamiltonian,
    pp_occupancy,
    ph_occupancy,
    lengths,
    partner,
    coupling,
    degeneracy,
    orbital,
):
    n = lax.axis_size("chan")
    m = lax.axis_size("blk")
    rows, columns = generator.shape[1:]
    widths = widths_of(columns)
    parts = len(widths)
    orbits = -(-NOB // 128) * 128
    anywhere = pl.BlockSpec(memory_space=pl.ANY)
    vmem = pl.BlockSpec(memory_space=pltpu.VMEM)
    smem = pl.BlockSpec(memory_space=pltpu.SMEM)
    dma = pltpu.SemaphoreType.DMA
    half = pltpu.VMEM((rows, columns), jnp.bfloat16)
    full = pltpu.VMEM((2 * rows, columns), jnp.bfloat16)
    cut = pltpu.VMEM((n, rows // n, columns), jnp.bfloat16)
    strips = [pltpu.VMEM((rows, w), jnp.bfloat16) for w in widths]
    cuts = [pltpu.VMEM((n, rows // n, w), jnp.bfloat16) for w in widths]
    scale = 1.0 / (8.0 * math.sqrt(n * columns / NOB))
    two_body, sums = pl.pallas_call(
        functools.partial(fused_kernel, n, m, widths, scale),
        out_shape=(
            jax.ShapeDtypeStruct((rows, columns), jnp.bfloat16),
            jax.ShapeDtypeStruct((1, orbits), jnp.float32),
        ),
        in_specs=[anywhere] * 2 + [vmem] * 2 + [smem] * 4 + [vmem],
        out_specs=(anywhere, vmem),
        scratch_shapes=[cut] * 4
        + [half] * 2
        + [full] * 2
        + [half] * 2
        + [
            pltpu.VMEM((rows, columns), jnp.float32),
            half,
            pltpu.VMEM((1, columns), jnp.float32),
            pltpu.VMEM((1, orbits), jnp.float32),
            pltpu.VMEM((n * m, 1, orbits), jnp.float32),
        ]
        + strips
        + cuts
        + [
            dma((2,)),
            dma((2,)),
            dma((2,)),
            dma((2, n)),
            dma((2, n)),
            dma((2, n)),
            dma((2, n)),
            dma((parts,)),
            dma((parts, n)),
            dma((parts, n)),
            dma((parts,)),
            dma((n * m,)),
            dma((n * m,)),
        ],
        compiler_params=pltpu.CompilerParams(
            collective_id=0, has_side_effects=True, vmem_limit_bytes=VMEM_LIMIT
        ),
        name="fused",
    )(
        generator.reshape(n, rows // n, columns),
        hamiltonian.reshape(n, rows // n, columns),
        pp_occupancy,
        ph_occupancy,
        partner[0],
        coupling[0],
        lengths,
        degeneracy,
        orbital,
    )
    return (two_body[None], sums[0, :NOB])


def solution(mesh):
    placed = (
        P("chan", "blk", None),
        P("chan", "blk", None),
        P("chan", None),
        P("chan", None),
        P("chan"),
        P("chan", None),
        P("chan", None),
        P("chan"),
        P("chan", "blk"),
    )
    n, m = mesh.shape["chan"], mesh.shape["blk"]

    def body(*args):
        rows, columns = args[0].shape[1:]
        tiled = m == 2 and n % 8 == 0 and rows % (16 * n) == 0 and columns % 256 == 0
        return (on_device if tiled else on_device_plain)(*args)

    return jax.shard_map(
        body,
        mesh=mesh,
        in_specs=placed,
        out_specs=(P("chan", "blk", None), P()),
        check_vma=False,
    )
```

```python
import functools
import math

import jax
import jax.numpy as jnp
from jax import lax
from jax.experimental import pallas as pl
from jax.experimental.pallas import tpu as pltpu
from jax.sharding import PartitionSpec as P

NOB = 240
MESH = pl.DeviceIdType.MESH
VMEM_LIMIT = 60 * 1024 * 1024


def scaled_copy(matrix, occupancy):
    return (matrix.astype(jnp.float32) * occupancy[None, :]).astype(jnp.bfloat16)


def make_fold(left_scaled, right_scaled, pieces):
    return jnp.dot(left_scaled, pieces[1], preferred_element_type=jnp.float32) - jnp.dot(
        right_scaled, pieces[0], preferred_element_type=jnp.float32
    )


def on_device_plain(
    generator,
    hamiltonian,
    pp_occupancy,
    ph_occupancy,
    lengths,
    partner,
    coupling,
    degeneracy,
    orbital,
):
    chan_count = lax.axis_size("chan")
    blk_index = lax.axis_index("blk")
    row_count = generator.shape[1]
    columns = generator.shape[2]
    piece_rows = row_count // chan_count
    col_ids = jnp.arange(columns, dtype=jnp.int32)
    row_ids = blk_index * row_count + jnp.arange(row_count, dtype=jnp.int32)
    live_mask = (row_ids[:, None] < lengths[0]) & (col_ids[None, :] < lengths[0])
    nothing = jnp.zeros((), jnp.bfloat16)
    gen_live = jnp.where(live_mask, generator[0], nothing)
    ham_live = jnp.where(live_mask, hamiltonian[0], nothing)
    gen_scaled = scaled_copy(gen_live, pp_occupancy[0])
    ham_scaled = scaled_copy(ham_live, pp_occupancy[0])
    owner_ids = jnp.arange(chan_count, dtype=jnp.int32)
    matches = partner[0][None, :] == owner_ids[:, None]
    sender_slot = jnp.sum(jnp.where(matches, owner_ids[None, :], 0), axis=1)
    scales = coupling[0]
    scales_slot = scales[sender_slot]
    ph_occ = ph_occupancy[0]
    gen_send = (
        gen_live.reshape(chan_count, piece_rows, columns)[sender_slot].astype(jnp.float32)
        * scales_slot[:, None, None]
    ).astype(jnp.bfloat16)
    ham_send = (
        ham_live.reshape(chan_count, piece_rows, columns)[sender_slot].astype(jnp.float32)
        * scales_slot[:, None, None]
    ).astype(jnp.bfloat16)
    gen_recv, ham_recv = (
        lax.all_to_all(gen_send, "chan", split_axis=0, concat_axis=0, tiled=True),
        lax.all_to_all(ham_send, "chan", split_axis=0, concat_axis=0, tiled=True),
    )
    ladder = make_fold(
        gen_scaled,
        ham_scaled,
        (
            lax.all_gather(gen_live, "blk", axis=0, tiled=True),
            lax.all_gather(ham_live, "blk", axis=0, tiled=True),
        ),
    )
    gen_rows = gen_recv.reshape(row_count, columns)
    ham_rows = ham_recv.reshape(row_count, columns)
    crossed = make_fold(
        scaled_copy(gen_rows, ph_occ),
        scaled_copy(ham_rows, ph_occ),
        (
            lax.all_gather(gen_rows, "blk", axis=0, tiled=True),
            lax.all_gather(ham_rows, "blk", axis=0, tiled=True),
        ),
    )
    crossed_back = crossed.astype(jnp.bfloat16).reshape(chan_count, piece_rows, columns)
    returned = lax.all_to_all(crossed_back, "chan", split_axis=0, concat_axis=0, tiled=True)
    restored = (returned[partner[0]].astype(jnp.float32) * scales[:, None, None]).reshape(
        row_count, columns
    )
    combined = jnp.where(live_mask, ladder + restored, jnp.zeros((), jnp.float32))
    two_body = combined.astype(jnp.bfloat16)[None]
    own_block = lax.dynamic_slice_in_dim(combined, blk_index * row_count, row_count, 1)
    weighted = jnp.diagonal(own_block) * degeneracy[0]
    orbit_match = orbital[0][:, None] == jnp.arange(NOB, dtype=jnp.int32)[None, :]
    partial_sums = jnp.sum(jnp.where(orbit_match, weighted[:, None], 0.0), axis=0)
    normalizer = 8.0 * math.sqrt(chan_count * columns / NOB)
    one_body = lax.psum(partial_sums, ("chan", "blk")) / normalizer
    return (two_body, one_body)


def widths_of(columns):
    unit = 256
    inner = columns - 2 * unit
    if inner <= 0 or inner % (2 * unit):
        return (unit,) * (columns // unit)
    return (unit,) + (2 * unit,) * (inner // (2 * unit)) + (unit,)


def fused_kernel(n, m, widths, scale, *refs):
    parts = len(widths)
    (
        gen_hbm,
        ham_hbm,
        pp_ref,
        ph_ref,
        partner_ref,
        coupling_ref,
        length_ref,
        weight_ref,
        orbital_ref,
        out,
        sum_ref,
        own_g,
        own_h,
        far_g,
        far_h,
        send_g,
        send_h,
        cross_g,
        cross_h,
        left,
        right,
        lad,
        diag,
        part,
        slots,
    ) = refs[:25]
    back = refs[25 : 25 + parts]
    ret = refs[25 + parts : 25 + 2 * parts]
    (
        own_sem,
        x_send,
        x_recv,
        a_send,
        a_recv,
        r_send,
        r_recv,
        l_sem,
        b_send,
        b_recv,
        t_send,
        t_recv,
    ) = refs[25 + 2 * parts :]
    c = lax.axis_index("chan")
    b = lax.axis_index("blk")
    ob = 1 - b
    me = c * m + b
    count = n * m
    piece, columns = gen_hbm.shape[1:]
    rows = n * piece
    orbits = part.shape[1]
    twin = (c, ob)
    ends = [sum(widths[: j + 1]) for j in range(parts)]
    starts = [
        pl.multiple_of((1 - b) * (ends[j] - widths[j]) + b * (columns - ends[j]), 128)
        for j in range(parts)
    ]
    middle = [end >= rows for end in ends].index(True)
    raw = ((gen_hbm, own_g, far_g), (ham_hbm, own_h, far_h))
    sent = ((send_g, cross_g), (send_h, cross_h))
    length = length_ref[0]

    def half_cols(half):
        return pl.ds(pl.multiple_of(half * rows, 128), rows)

    def slot(half, d):
        return pl.ds(pl.multiple_of((half * n + d) * piece, piece), piece)

    def strip(d):
        return pl.ds(pl.multiple_of(d * piece, piece), piece)

    level = n // 4
    z, y, x = c // level, c % level // 2, c % 2

    def chip(to, turn):
        return to * level + (y + turn // 2) % (level // 2) * 2 + (x + turn) % 2

    def pick(i, first, second, third):
        q, r = i // level, i % level
        own = q // 3
        to = first * ((1 - q) * (2 - q) // 2) + second * (q * (2 - q)) + third * (q * (q - 1) // 2)
        turn = r + b * (level - 1 - 2 * r)
        return chip(to * (1 - own) + z * own, turn * (1 - own) + (r + 1) * own)

    def target(i):
        return pick(i, 1 + z % 2, 3 * (1 - z % 2), (z + 2) % 4)

    def giver(i):
        return pick(i, 3 * (1 - z // 2), 2 - z // 2, z + 1 - 2 * (z % 2))

    def source(i):
        return pick(i, z + 1 - 2 * (z % 2), 2 - z // 2, 3 * (1 - z // 2))

    def each(count, body, first=0):
        def step(i, carry):
            body(i)
            return carry

        lax.fori_loop(first, count, step, 0)

    def own_copy(t):
        return pltpu.make_async_copy(raw[t][0], raw[t][1], own_sem.at[t])

    def twin_copy(t):
        return pltpu.make_async_remote_copy(
            src_ref=raw[t][0],
            dst_ref=raw[t][2],
            send_sem=x_send.at[t],
            recv_sem=x_recv.at[t],
            device_id=twin,
            device_id_type=MESH,
        )

    def piece_copy(t, k, d):
        return pltpu.make_async_remote_copy(
            src_ref=sent[t][0].at[strip(k)],
            dst_ref=sent[t][1].at[slot(b, d)],
            send_sem=a_send.at[t, k],
            recv_sem=a_recv.at[t, d],
            device_id=(k, b),
            device_id_type=MESH,
        )

    def relay(t, half, d):
        return pltpu.make_async_remote_copy(
            src_ref=sent[t][1].at[slot(half, d)],
            dst_ref=sent[t][1].at[slot(half, d)],
            send_sem=r_send.at[t, d],
            recv_sem=r_recv.at[t, d],
            device_id=twin,
            device_id_type=MESH,
        )

    def back_copy(j, k, d):
        return pltpu.make_async_remote_copy(
            src_ref=back[j].at[strip(k)],
            dst_ref=ret[j].at[d],
            send_sem=b_send.at[j, k],
            recv_sem=b_recv.at[j, d],
            device_id=(k, b),
            device_id_type=MESH,
        )

    def back_local(j):
        return pltpu.make_async_copy(back[j].at[strip(c)], ret[j].at[c], l_sem.at[j])

    def peer(i):
        return (me + 1 + i) % count

    def total_copy(to, origin):
        return pltpu.make_async_remote_copy(
            src_ref=part,
            dst_ref=slots.at[origin],
            send_sem=t_send.at[to],
            recv_sem=t_recv.at[origin],
            device_id=(to // m, to % m),
            device_id_type=MESH,
        )

    for t in range(2):
        own_copy(t).start()
    barrier = pltpu.get_barrier_semaphore()

    def greet(i):
        for core in range(m):
            pl.semaphore_signal(barrier, inc=1, device_id=(giver(i), core), device_id_type=MESH)

    each(n - 1, greet)
    pl.semaphore_signal(barrier, inc=1, device_id=twin, device_id_type=MESH)
    for t in range(2):
        own_copy(t).wait()

    col_live = lax.broadcasted_iota(jnp.int32, (1, columns), 1) < length
    row_ids = lax.broadcasted_iota(jnp.int32, (piece, 1), 0)

    def prepare(k, refs_at):
        p, weight = jnp.int32(0), jnp.float32(0.0)
        for q in range(n):
            match = partner_ref[q] == k
            p = jnp.where(match, q, p)
            weight = jnp.where(match, coupling_ref[q], weight)
        factor = jnp.where(col_live, weight, 0.0)
        factor = jnp.where(row_ids + (b * n + p) * piece < length, factor, 0.0)
        for t in range(2):
            dst, where = refs_at[t]
            dst[where, :] = (raw[t][1][p].astype(jnp.float32) * factor).astype(jnp.bfloat16)

    def prepare_sent(i):
        k = target(i)
        prepare(k, [(send_g, strip(k)), (send_h, strip(k))])

    def send(i):
        k = target(i)
        for t in range(2):
            piece_copy(t, k, c).start()

    ahead = 2
    each(ahead, prepare_sent)
    pl.semaphore_wait(barrier, count - 1)
    distant = n - level

    def send_and_prepare(i):
        send(i)
        prepare_sent(i + ahead)

    each(distant - ahead, send_and_prepare)
    each(distant, send, distant - ahead)
    prepare(c, [(cross_g, slot(b, c)), (cross_h, slot(b, c))])
    for t in range(2):
        twin_copy(t).start()
    each(n - 1, prepare_sent, distant)

    def pp_scale(i):
        factor = jnp.where(col_live, pp_ref[...], 0.0)
        left[strip(i), :] = (own_g[i].astype(jnp.float32) * factor).astype(jnp.bfloat16)
        right[strip(i), :] = (own_h[i].astype(jnp.float32) * factor).astype(jnp.bfloat16)

    each(n, pp_scale)

    def dot(x, y):
        return jnp.dot(x, y, preferred_element_type=jnp.float32)

    for t in range(2):
        relay(t, b, c).start()
        twin_copy(t).wait_recv()
    unit = 256

    def ladder_step(j):
        cols = pl.ds(pl.multiple_of(j * unit, unit), unit)
        near, other = half_cols(b), half_cols(ob)
        lad[:, cols] = (
            dot(left[:, near], own_h[:, :, cols].reshape(rows, unit))
            + dot(left[:, other], far_h[:, :, cols].reshape(rows, unit))
            - dot(right[:, near], own_g[:, :, cols].reshape(rows, unit))
            - dot(right[:, other], far_g[:, :, cols].reshape(rows, unit))
        )

    each(columns // unit, ladder_step)
    each(n - 1, send, distant)

    def ph_scale(d):
        factor = ph_ref[...]
        left[strip(d), :] = (cross_g[slot(b, d), :].astype(jnp.float32) * factor).astype(jnp.bfloat16)
        right[strip(d), :] = (cross_h[slot(b, d), :].astype(jnp.float32) * factor).astype(jnp.bfloat16)

    ph_scale(c)

    def take(i):
        d = source(i)
        for t in range(2):
            piece_copy(t, d, d).wait_recv()
            relay(t, b, d).start()
        ph_scale(d)

    each(n - 1, take)

    def take_relay(d):
        for t in range(2):
            relay(t, ob, d).wait_recv()

    each(n, take_relay)

    for j in range(parts):
        cols = pl.ds(starts[j], widths[j])
        back[j][...] = (dot(left[...], cross_h[:, cols]) - dot(right[...], cross_g[:, cols])).astype(
            jnp.bfloat16
        )

        def give(i, j=j):
            back_copy(j, giver(i), c).start()

        each(n - 1, give)
        back_local(j).start()

    first = b * rows
    for j in range(parts):

        def take_back(i, j=j):
            d = source(i)
            back_copy(j, d, d).wait_recv()

        each(n - 1, take_back)
        back_local(j).wait()
        cols = pl.ds(starts[j], widths[j])
        col_ids = starts[j] + lax.broadcasted_iota(jnp.int32, (1, widths[j]), 1)
        diag[:, cols] = jnp.zeros((1, widths[j]), jnp.float32)

        def fold(p, j=j, cols=cols, col_ids=col_ids):
            ids = row_ids + (first + p * piece)
            value = lad[strip(p), cols] + ret[j][partner_ref[p]].astype(jnp.float32) * coupling_ref[p]
            value = jnp.where((ids < length) & (col_ids < length), value, 0.0)
            out[strip(p), cols] = value.astype(jnp.bfloat16)
            diag[:, cols] += jnp.sum(jnp.where(ids == col_ids, value, 0.0), axis=0, keepdims=True)

        each(n, fold)
        if j != middle:
            continue
        weighted = diag[:, half_cols(b)] * weight_ref[0]
        hits = lax.broadcasted_iota(jnp.int32, (orbits, rows), 0) == orbital_ref[...]
        part[...] = lax.dot_general(
            weighted,
            jnp.where(hits, 1.0, 0.0),
            (((1,), (1,)), ((), ())),
            precision=lax.Precision.HIGHEST,
            preferred_element_type=jnp.float32,
        )

        def total_send(i):
            total_copy(peer(i), me).start()

        each(count - 1, total_send)
        slots[me] = part[...]

    for t in range(2):
        twin_copy(t).wait_send()

    def drain(i):
        k = target(i)
        for t in range(2):
            piece_copy(t, k, c).wait_send()
        for j in range(parts):
            back_copy(j, k, c).wait_send()

    each(n - 1, drain)

    def drain_relay(d):
        for t in range(2):
            relay(t, b, d).wait_send()

    each(n, drain_relay)

    def total_take(i):
        other = peer(i)
        total_copy(other, me).wait_send()
        total_copy(other, other).wait_recv()

    each(count - 1, total_take)
    sum_ref[...] = jnp.sum(slots[...], axis=0) * scale


def on_device(
    generator,
    hamiltonian,
    pp_occupancy,
    ph_occupancy,
    lengths,
    partner,
    coupling,
    degeneracy,
    orbital,
):
    n = lax.axis_size("chan")
    m = lax.axis_size("blk")
    rows, columns = generator.shape[1:]
    widths = widths_of(columns)
    parts = len(widths)
    orbits = -(-NOB // 128) * 128
    anywhere = pl.BlockSpec(memory_space=pl.ANY)
    vmem = pl.BlockSpec(memory_space=pltpu.VMEM)
    smem = pl.BlockSpec(memory_space=pltpu.SMEM)
    dma = pltpu.SemaphoreType.DMA
    half = pltpu.VMEM((rows, columns), jnp.bfloat16)
    full = pltpu.VMEM((2 * rows, columns), jnp.bfloat16)
    cut = pltpu.VMEM((n, rows // n, columns), jnp.bfloat16)
    strips = [pltpu.VMEM((rows, w), jnp.bfloat16) for w in widths]
    cuts = [pltpu.VMEM((n, rows // n, w), jnp.bfloat16) for w in widths]
    scale = 1.0 / (8.0 * math.sqrt(n * columns / NOB))
    two_body, sums = pl.pallas_call(
        functools.partial(fused_kernel, n, m, widths, scale),
        out_shape=(
            pltpu.VMEM((rows, columns), jnp.bfloat16),
            pltpu.VMEM((1, orbits), jnp.float32),
        ),
        in_specs=[anywhere] * 2 + [vmem] * 2 + [smem] * 4 + [vmem],
        out_specs=(vmem, vmem),
        scratch_shapes=[cut] * 4
        + [half] * 2
        + [full] * 2
        + [half] * 2
        + [
            pltpu.VMEM((rows, columns), jnp.float32),
            pltpu.VMEM((1, columns), jnp.float32),
            pltpu.VMEM((1, orbits), jnp.float32),
            pltpu.VMEM((n * m, 1, orbits), jnp.float32),
        ]
        + strips
        + cuts
        + [
            dma((2,)),
            dma((2,)),
            dma((2,)),
            dma((2, n)),
            dma((2, n)),
            dma((2, n)),
            dma((2, n)),
            dma((parts,)),
            dma((parts, n)),
            dma((parts, n)),
            dma((n * m,)),
            dma((n * m,)),
        ],
        compiler_params=pltpu.CompilerParams(
            collective_id=0, has_side_effects=True, vmem_limit_bytes=VMEM_LIMIT
        ),
        name="fused",
    )(
        generator.reshape(n, rows // n, columns),
        hamiltonian.reshape(n, rows // n, columns),
        pp_occupancy,
        ph_occupancy,
        partner[0],
        coupling[0],
        lengths,
        degeneracy,
        orbital,
    )
    return (two_body[None], sums[0, :NOB])


def solution(mesh):
    placed = (
        P("chan", "blk", None),
        P("chan", "blk", None),
        P("chan", None),
        P("chan", None),
        P("chan"),
        P("chan", None),
        P("chan", None),
        P("chan"),
        P("chan", "blk"),
    )
    n, m = mesh.shape["chan"], mesh.shape["blk"]

    def body(*args):
        rows, columns = args[0].shape[1:]
        tiled = m == 2 and n % 8 == 0 and rows % (16 * n) == 0 and columns % 256 == 0
        return (on_device if tiled else on_device_plain)(*args)

    return jax.shard_map(
        body,
        mesh=mesh,
        in_specs=placed,
        out_specs=(P("chan", "blk", None), P()),
        check_vma=False,
    )
```

```python
import functools
import math

import jax
import jax.numpy as jnp
from jax import lax
from jax.experimental import pallas as pl
from jax.experimental.pallas import tpu as pltpu
from jax.sharding import PartitionSpec as P

NOB = 240
MESH = pl.DeviceIdType.MESH
VMEM_LIMIT = 60 * 1024 * 1024


def scaled_copy(matrix, occupancy):
    return (matrix.astype(jnp.float32) * occupancy[None, :]).astype(jnp.bfloat16)


def make_fold(left_scaled, right_scaled, pieces):
    return jnp.dot(left_scaled, pieces[1], preferred_element_type=jnp.float32) - jnp.dot(
        right_scaled, pieces[0], preferred_element_type=jnp.float32
    )


def on_device_plain(
    generator,
    hamiltonian,
    pp_occupancy,
    ph_occupancy,
    lengths,
    partner,
    coupling,
    degeneracy,
    orbital,
):
    chan_count = lax.axis_size("chan")
    blk_index = lax.axis_index("blk")
    row_count = generator.shape[1]
    columns = generator.shape[2]
    piece_rows = row_count // chan_count
    col_ids = jnp.arange(columns, dtype=jnp.int32)
    row_ids = blk_index * row_count + jnp.arange(row_count, dtype=jnp.int32)
    live_mask = (row_ids[:, None] < lengths[0]) & (col_ids[None, :] < lengths[0])
    nothing = jnp.zeros((), jnp.bfloat16)
    gen_live = jnp.where(live_mask, generator[0], nothing)
    ham_live = jnp.where(live_mask, hamiltonian[0], nothing)
    gen_scaled = scaled_copy(gen_live, pp_occupancy[0])
    ham_scaled = scaled_copy(ham_live, pp_occupancy[0])
    owner_ids = jnp.arange(chan_count, dtype=jnp.int32)
    matches = partner[0][None, :] == owner_ids[:, None]
    sender_slot = jnp.sum(jnp.where(matches, owner_ids[None, :], 0), axis=1)
    scales = coupling[0]
    scales_slot = scales[sender_slot]
    ph_occ = ph_occupancy[0]
    gen_send = (
        gen_live.reshape(chan_count, piece_rows, columns)[sender_slot].astype(jnp.float32)
        * scales_slot[:, None, None]
    ).astype(jnp.bfloat16)
    ham_send = (
        ham_live.reshape(chan_count, piece_rows, columns)[sender_slot].astype(jnp.float32)
        * scales_slot[:, None, None]
    ).astype(jnp.bfloat16)
    gen_recv, ham_recv = (
        lax.all_to_all(gen_send, "chan", split_axis=0, concat_axis=0, tiled=True),
        lax.all_to_all(ham_send, "chan", split_axis=0, concat_axis=0, tiled=True),
    )
    ladder = make_fold(
        gen_scaled,
        ham_scaled,
        (
            lax.all_gather(gen_live, "blk", axis=0, tiled=True),
            lax.all_gather(ham_live, "blk", axis=0, tiled=True),
        ),
    )
    gen_rows = gen_recv.reshape(row_count, columns)
    ham_rows = ham_recv.reshape(row_count, columns)
    crossed = make_fold(
        scaled_copy(gen_rows, ph_occ),
        scaled_copy(ham_rows, ph_occ),
        (
            lax.all_gather(gen_rows, "blk", axis=0, tiled=True),
            lax.all_gather(ham_rows, "blk", axis=0, tiled=True),
        ),
    )
    crossed_back = crossed.astype(jnp.bfloat16).reshape(chan_count, piece_rows, columns)
    returned = lax.all_to_all(crossed_back, "chan", split_axis=0, concat_axis=0, tiled=True)
    restored = (returned[partner[0]].astype(jnp.float32) * scales[:, None, None]).reshape(
        row_count, columns
    )
    combined = jnp.where(live_mask, ladder + restored, jnp.zeros((), jnp.float32))
    two_body = combined.astype(jnp.bfloat16)[None]
    own_block = lax.dynamic_slice_in_dim(combined, blk_index * row_count, row_count, 1)
    weighted = jnp.diagonal(own_block) * degeneracy[0]
    orbit_match = orbital[0][:, None] == jnp.arange(NOB, dtype=jnp.int32)[None, :]
    partial_sums = jnp.sum(jnp.where(orbit_match, weighted[:, None], 0.0), axis=0)
    normalizer = 8.0 * math.sqrt(chan_count * columns / NOB)
    one_body = lax.psum(partial_sums, ("chan", "blk")) / normalizer
    return (two_body, one_body)


def widths_of(columns):
    unit = 256
    inner = columns - 2 * unit
    if inner <= 0 or inner % (2 * unit):
        return (unit,) * (columns // unit)
    return (unit,) + (2 * unit,) * (inner // (2 * unit)) + (unit,)


def fused_kernel(n, m, widths, scale, *refs):
    parts = len(widths)
    (
        gen_hbm,
        ham_hbm,
        pp_hbm,
        ph_hbm,
        partner_hbm,
        coupling_hbm,
        length_hbm,
        weight_hbm,
        orbital_hbm,
        out,
        sum_ref,
        pp_ref,
        ph_ref,
        partner_ref,
        coupling_ref,
        length_ref,
        weight_ref,
        orbital_ref,
        own_g,
        own_h,
        far_g,
        far_h,
        send_g,
        send_h,
        cross_g,
        cross_h,
        left,
        right,
        lad,
        diag,
        part,
        slots,
    ) = refs[:32]
    back = refs[32 : 32 + parts]
    ret = refs[32 + parts : 32 + 2 * parts]
    (
        small_sem,
        own_sem,
        x_send,
        x_recv,
        a_send,
        a_recv,
        r_send,
        r_recv,
        l_sem,
        b_send,
        b_recv,
        t_send,
        t_recv,
    ) = refs[32 + 2 * parts :]
    c = lax.axis_index("chan")
    b = lax.axis_index("blk")
    ob = 1 - b
    me = c * m + b
    count = n * m
    piece, columns = gen_hbm.shape[1:]
    rows = n * piece
    orbits = part.shape[1]
    twin = (c, ob)
    ends = [sum(widths[: j + 1]) for j in range(parts)]
    starts = [
        pl.multiple_of((1 - b) * (ends[j] - widths[j]) + b * (columns - ends[j]), 128)
        for j in range(parts)
    ]
    middle = [end >= rows for end in ends].index(True)
    raw = ((gen_hbm, own_g, far_g), (ham_hbm, own_h, far_h))
    sent = ((send_g, cross_g), (send_h, cross_h))
    small = (
        (pp_hbm, pp_ref),
        (ph_hbm, ph_ref),
        (partner_hbm, partner_ref),
        (coupling_hbm, coupling_ref),
        (length_hbm, length_ref),
        (weight_hbm, weight_ref),
        (orbital_hbm, orbital_ref),
    )

    def half_cols(half):
        return pl.ds(pl.multiple_of(half * rows, 128), rows)

    def slot(half, d):
        return pl.ds(pl.multiple_of((half * n + d) * piece, piece), piece)

    def strip(d):
        return pl.ds(pl.multiple_of(d * piece, piece), piece)

    level = n // 4
    z, y, x = c // level, c % level // 2, c % 2

    def chip(to, turn):
        return to * level + (y + turn // 2) % (level // 2) * 2 + (x + turn) % 2

    def pick(i, first, second, third):
        q, r = i // level, i % level
        own = q // 3
        to = first * ((1 - q) * (2 - q) // 2) + second * (q * (2 - q)) + third * (q * (q - 1) // 2)
        turn = r + b * (level - 1 - 2 * r)
        return chip(to * (1 - own) + z * own, turn * (1 - own) + (r + 1) * own)

    def target(i):
        return pick(i, 1 + z % 2, 3 * (1 - z % 2), (z + 2) % 4)

    def giver(i):
        return pick(i, 3 * (1 - z // 2), 2 - z // 2, z + 1 - 2 * (z % 2))

    def source(i):
        return pick(i, z + 1 - 2 * (z % 2), 2 - z // 2, 3 * (1 - z // 2))

    def each(count, body, first=0):
        def step(i, carry):
            body(i)
            return carry

        lax.fori_loop(first, count, step, 0)

    def small_copy(i):
        return pltpu.make_async_copy(small[i][0], small[i][1], small_sem.at[i])

    def own_copy(t):
        return pltpu.make_async_copy(raw[t][0], raw[t][1], own_sem.at[t])

    def twin_copy(t):
        return pltpu.make_async_remote_copy(
            src_ref=raw[t][0],
            dst_ref=raw[t][2],
            send_sem=x_send.at[t],
            recv_sem=x_recv.at[t],
            device_id=twin,
            device_id_type=MESH,
        )

    def piece_copy(t, k, d):
        return pltpu.make_async_remote_copy(
            src_ref=sent[t][0].at[strip(k)],
            dst_ref=sent[t][1].at[slot(b, d)],
            send_sem=a_send.at[t],
            recv_sem=a_recv.at[t, d],
            device_id=(k, b),
            device_id_type=MESH,
        )

    def relay(t, half, d):
        return pltpu.make_async_remote_copy(
            src_ref=sent[t][1].at[slot(half, d)],
            dst_ref=sent[t][1].at[slot(half, d)],
            send_sem=r_send.at[t],
            recv_sem=r_recv.at[t],
            device_id=twin,
            device_id_type=MESH,
        )

    def back_copy(j, k, d):
        return pltpu.make_async_remote_copy(
            src_ref=back[j].at[strip(k)],
            dst_ref=ret[j].at[d],
            send_sem=b_send.at[j],
            recv_sem=b_recv.at[j],
            device_id=(k, b),
            device_id_type=MESH,
        )

    others = pl.ds(0, (n - 1) * piece)

    def all_pieces(t):
        return pltpu.make_async_remote_copy(
            src_ref=sent[t][0].at[others],
            dst_ref=sent[t][1].at[others],
            send_sem=a_send.at[t],
            recv_sem=r_recv.at[t],
            device_id=twin,
            device_id_type=MESH,
        )

    def all_relays(t):
        where = pl.ds(pl.multiple_of(ob * rows, rows), rows)
        return pltpu.make_async_remote_copy(
            src_ref=sent[t][1].at[where],
            dst_ref=sent[t][1].at[where],
            send_sem=r_send.at[t],
            recv_sem=r_recv.at[t],
            device_id=twin,
            device_id_type=MESH,
        )

    def all_back(j):
        return pltpu.make_async_remote_copy(
            src_ref=back[j].at[others],
            dst_ref=ret[j].at[pl.ds(0, n - 1)],
            send_sem=b_send.at[j],
            recv_sem=b_recv.at[j],
            device_id=twin,
            device_id_type=MESH,
        )

    def back_local(j):
        return pltpu.make_async_copy(back[j].at[strip(c)], ret[j].at[c], l_sem.at[j])

    def peer(i):
        return (me + 1 + i) % count

    def total_copy(to, origin):
        return pltpu.make_async_remote_copy(
            src_ref=part,
            dst_ref=slots.at[origin],
            send_sem=t_send.at[to],
            recv_sem=t_recv.at[origin],
            device_id=(to // m, to % m),
            device_id_type=MESH,
        )

    for i in range(len(small)):
        small_copy(i).start()
    for t in range(2):
        own_copy(t).start()
    barrier = pltpu.get_barrier_semaphore()

    def greet(i):
        for core in range(m):
            pl.semaphore_signal(barrier, inc=1, device_id=(giver(i), core), device_id_type=MESH)

    each(n - 1, greet)
    pl.semaphore_signal(barrier, inc=1, device_id=twin, device_id_type=MESH)
    for i in range(len(small)):
        small_copy(i).wait()
    for t in range(2):
        own_copy(t).wait()
    length = length_ref[...]

    col_live = lax.broadcasted_iota(jnp.int32, (1, columns), 1) < length
    row_ids = lax.broadcasted_iota(jnp.int32, (piece, 1), 0)

    def prepare(k, refs_at):
        p, weight = jnp.int32(0), jnp.float32(0.0)
        for q in range(n):
            match = partner_ref[q] == k
            p = jnp.where(match, q, p)
            weight = jnp.where(match, coupling_ref[q], weight)
        factor = jnp.where(col_live, weight, 0.0)
        factor = jnp.where(row_ids + (b * n + p) * piece < length, factor, 0.0)
        for t in range(2):
            dst, where = refs_at[t]
            dst[where, :] = (raw[t][1][p].astype(jnp.float32) * factor).astype(jnp.bfloat16)

    def prepare_sent(i):
        k = target(i)
        prepare(k, [(send_g, strip(k)), (send_h, strip(k))])

    def send(i):
        k = target(i)
        for t in range(2):
            piece_copy(t, k, c).start()

    ahead = 2
    each(ahead, prepare_sent)
    pl.semaphore_wait(barrier, count - 1)
    distant = n - level

    def send_and_prepare(i):
        send(i)
        prepare_sent(i + ahead)

    each(distant - ahead, send_and_prepare)
    each(distant, send, distant - ahead)
    prepare(c, [(cross_g, slot(b, c)), (cross_h, slot(b, c))])
    for t in range(2):
        twin_copy(t).start()
    each(n - 1, prepare_sent, distant)

    def pp_scale(i):
        factor = jnp.where(col_live, pp_ref[...], 0.0)
        left[strip(i), :] = (own_g[i].astype(jnp.float32) * factor).astype(jnp.bfloat16)
        right[strip(i), :] = (own_h[i].astype(jnp.float32) * factor).astype(jnp.bfloat16)

    each(n, pp_scale)

    def dot(x, y):
        return jnp.dot(x, y, preferred_element_type=jnp.float32)

    for t in range(2):
        relay(t, b, c).start()
        twin_copy(t).wait_recv()
    unit = 256

    def ladder_step(j):
        cols = pl.ds(pl.multiple_of(j * unit, unit), unit)
        near, other = half_cols(b), half_cols(ob)
        lad[:, cols] = (
            dot(left[:, near], own_h[:, :, cols].reshape(rows, unit))
            + dot(left[:, other], far_h[:, :, cols].reshape(rows, unit))
            - dot(right[:, near], own_g[:, :, cols].reshape(rows, unit))
            - dot(right[:, other], far_g[:, :, cols].reshape(rows, unit))
        )

    each(columns // unit, ladder_step)
    each(n - 1, send, distant)

    def ph_scale(d):
        factor = ph_ref[...]
        left[strip(d), :] = (cross_g[slot(b, d), :].astype(jnp.float32) * factor).astype(jnp.bfloat16)
        right[strip(d), :] = (cross_h[slot(b, d), :].astype(jnp.float32) * factor).astype(jnp.bfloat16)

    ph_scale(c)

    def take(i):
        d = source(i)
        for t in range(2):
            piece_copy(t, d, d).wait_recv()
            relay(t, b, d).start()
        ph_scale(d)

    each(n - 1, take)

    for t in range(2):
        all_relays(t).wait_recv()

    for j in range(parts):
        cols = pl.ds(starts[j], widths[j])
        back[j][...] = (dot(left[...], cross_h[:, cols]) - dot(right[...], cross_g[:, cols])).astype(
            jnp.bfloat16
        )

        def give(i, j=j):
            back_copy(j, giver(i), c).start()

        each(n - 1, give)
        back_local(j).start()

    for t in range(2):
        twin_copy(t).wait_send()
        all_pieces(t).wait_send()
        all_relays(t).wait_send()

    def total_take(i):
        other = peer(i)
        total_copy(other, me).wait_send()
        total_copy(other, other).wait_recv()

    first = b * rows
    for j in range(parts):
        if j + 1 == parts:
            each(count - 1, total_take)
            sum_ref[...] = jnp.sum(slots[...], axis=0) * scale
            for i in range(j):
                all_back(i).wait_send()
        all_back(j).wait_recv()
        back_local(j).wait()
        cols = pl.ds(starts[j], widths[j])
        col_ids = starts[j] + lax.broadcasted_iota(jnp.int32, (1, widths[j]), 1)
        if j <= middle:
            diag[:, cols] = jnp.zeros((1, widths[j]), jnp.float32)

        def fold(p, j=j, cols=cols, col_ids=col_ids):
            ids = row_ids + (first + p * piece)
            value = lad[strip(p), cols] + ret[j][partner_ref[p]].astype(jnp.float32) * coupling_ref[p]
            value = jnp.where((ids < length) & (col_ids < length), value, 0.0)
            out[strip(p), cols] = value.astype(jnp.bfloat16)
            if j <= middle:
                diag[:, cols] += jnp.sum(jnp.where(ids == col_ids, value, 0.0), axis=0, keepdims=True)

        each(n, fold)
        if j != middle:
            continue
        weighted = diag[:, half_cols(b)] * weight_ref[...]
        hits = lax.broadcasted_iota(jnp.int32, (orbits, rows), 0) == orbital_ref[...]
        part[...] = lax.dot_general(
            weighted,
            jnp.where(hits, 1.0, 0.0),
            (((1,), (1,)), ((), ())),
            precision=lax.Precision.HIGHEST,
            preferred_element_type=jnp.float32,
        )

        def total_send(i):
            total_copy(peer(i), me).start()

        each(count - 1, total_send)
        slots[me] = part[...]

    all_back(parts - 1).wait_send()


def on_device(
    generator,
    hamiltonian,
    pp_occupancy,
    ph_occupancy,
    lengths,
    partner,
    coupling,
    degeneracy,
    orbital,
):
    n = lax.axis_size("chan")
    m = lax.axis_size("blk")
    rows, columns = generator.shape[1:]
    widths = widths_of(columns)
    parts = len(widths)
    orbits = -(-NOB // 128) * 128
    anywhere = pl.BlockSpec(memory_space=pl.ANY)
    hbm = pl.BlockSpec(memory_space=pltpu.HBM)
    vmem = pl.BlockSpec(memory_space=pltpu.VMEM)
    dma = pltpu.SemaphoreType.DMA
    half = pltpu.VMEM((rows, columns), jnp.bfloat16)
    full = pltpu.VMEM((2 * rows, columns), jnp.bfloat16)
    cut = pltpu.VMEM((n, rows // n, columns), jnp.bfloat16)
    strips = [pltpu.VMEM((rows, w), jnp.bfloat16) for w in widths]
    cuts = [pltpu.VMEM((n, rows // n, w), jnp.bfloat16) for w in widths]
    scale = 1.0 / (8.0 * math.sqrt(n * columns / NOB))
    two_body, sums = pl.pallas_call(
        functools.partial(fused_kernel, n, m, widths, scale),
        out_shape=(
            pltpu.VMEM((rows, columns), jnp.bfloat16),
            pltpu.VMEM((1, orbits), jnp.float32),
        ),
        in_specs=[anywhere] * 2 + [hbm] * 7,
        out_specs=(vmem, vmem),
        scratch_shapes=[
            pltpu.VMEM((1, columns), jnp.float32),
            pltpu.VMEM((1, columns), jnp.float32),
            pltpu.SMEM((n,), jnp.int32),
            pltpu.SMEM((n,), jnp.float32),
            pltpu.VMEM((1, 1), jnp.int32),
            pltpu.VMEM((1, 1), jnp.float32),
            pltpu.VMEM((1, rows), jnp.int32),
        ]
        + [cut] * 4
        + [half] * 2
        + [full] * 2
        + [half] * 2
        + [
            pltpu.VMEM((rows, columns), jnp.float32),
            pltpu.VMEM((1, columns), jnp.float32),
            pltpu.VMEM((1, orbits), jnp.float32),
            pltpu.VMEM((n * m, 1, orbits), jnp.float32),
        ]
        + strips
        + cuts
        + [
            dma((7,)),
            dma((2,)),
            dma((2,)),
            dma((2,)),
            dma((2,)),
            dma((2, n)),
            dma((2,)),
            dma((2,)),
            dma((parts,)),
            dma((parts,)),
            dma((parts,)),
            dma((n * m,)),
            dma((n * m,)),
        ],
        compiler_params=pltpu.CompilerParams(
            collective_id=0, has_side_effects=True, vmem_limit_bytes=VMEM_LIMIT
        ),
        name="fused",
    )(
        generator.reshape(n, rows // n, columns),
        hamiltonian.reshape(n, rows // n, columns),
        pp_occupancy,
        ph_occupancy,
        partner[0],
        coupling[0],
        lengths[None],
        degeneracy[None],
        orbital,
    )
    return (two_body[None], sums[0, :NOB])


def solution(mesh):
    placed = (
        P("chan", "blk", None),
        P("chan", "blk", None),
        P("chan", None),
        P("chan", None),
        P("chan"),
        P("chan", None),
        P("chan", None),
        P("chan"),
        P("chan", "blk"),
    )
    n, m = mesh.shape["chan"], mesh.shape["blk"]

    def body(*args):
        rows, columns = args[0].shape[1:]
        tiled = m == 2 and n % 8 == 0 and rows % (16 * n) == 0 and columns % 256 == 0
        return (on_device if tiled else on_device_plain)(*args)

    return jax.shard_map(
        body,
        mesh=mesh,
        in_specs=placed,
        out_specs=(P("chan", "blk", None), P()),
        check_vma=False,
    )
```

```python
import functools
import math

import jax
import jax.numpy as jnp
from jax import lax
from jax.experimental import pallas as pl
from jax.experimental.pallas import tpu as pltpu
from jax.sharding import PartitionSpec as P

NOB = 240
MESH = pl.DeviceIdType.MESH
VMEM_LIMIT = 60 * 1024 * 1024


def scaled_copy(matrix, occupancy):
    return (matrix.astype(jnp.float32) * occupancy[None, :]).astype(jnp.bfloat16)


def make_fold(left_scaled, right_scaled, pieces):
    return jnp.dot(left_scaled, pieces[1], preferred_element_type=jnp.float32) - jnp.dot(
        right_scaled, pieces[0], preferred_element_type=jnp.float32
    )


def on_device_plain(
    generator,
    hamiltonian,
    pp_occupancy,
    ph_occupancy,
    lengths,
    partner,
    coupling,
    degeneracy,
    orbital,
):
    chan_count = lax.axis_size("chan")
    blk_index = lax.axis_index("blk")
    row_count = generator.shape[1]
    columns = generator.shape[2]
    piece_rows = row_count // chan_count
    col_ids = jnp.arange(columns, dtype=jnp.int32)
    row_ids = blk_index * row_count + jnp.arange(row_count, dtype=jnp.int32)
    live_mask = (row_ids[:, None] < lengths[0]) & (col_ids[None, :] < lengths[0])
    nothing = jnp.zeros((), jnp.bfloat16)
    gen_live = jnp.where(live_mask, generator[0], nothing)
    ham_live = jnp.where(live_mask, hamiltonian[0], nothing)
    gen_scaled = scaled_copy(gen_live, pp_occupancy[0])
    ham_scaled = scaled_copy(ham_live, pp_occupancy[0])
    owner_ids = jnp.arange(chan_count, dtype=jnp.int32)
    matches = partner[0][None, :] == owner_ids[:, None]
    sender_slot = jnp.sum(jnp.where(matches, owner_ids[None, :], 0), axis=1)
    scales = coupling[0]
    scales_slot = scales[sender_slot]
    ph_occ = ph_occupancy[0]
    gen_send = (
        gen_live.reshape(chan_count, piece_rows, columns)[sender_slot].astype(jnp.float32)
        * scales_slot[:, None, None]
    ).astype(jnp.bfloat16)
    ham_send = (
        ham_live.reshape(chan_count, piece_rows, columns)[sender_slot].astype(jnp.float32)
        * scales_slot[:, None, None]
    ).astype(jnp.bfloat16)
    gen_recv, ham_recv = (
        lax.all_to_all(gen_send, "chan", split_axis=0, concat_axis=0, tiled=True),
        lax.all_to_all(ham_send, "chan", split_axis=0, concat_axis=0, tiled=True),
    )
    ladder = make_fold(
        gen_scaled,
        ham_scaled,
        (
            lax.all_gather(gen_live, "blk", axis=0, tiled=True),
            lax.all_gather(ham_live, "blk", axis=0, tiled=True),
        ),
    )
    gen_rows = gen_recv.reshape(row_count, columns)
    ham_rows = ham_recv.reshape(row_count, columns)
    crossed = make_fold(
        scaled_copy(gen_rows, ph_occ),
        scaled_copy(ham_rows, ph_occ),
        (
            lax.all_gather(gen_rows, "blk", axis=0, tiled=True),
            lax.all_gather(ham_rows, "blk", axis=0, tiled=True),
        ),
    )
    crossed_back = crossed.astype(jnp.bfloat16).reshape(chan_count, piece_rows, columns)
    returned = lax.all_to_all(crossed_back, "chan", split_axis=0, concat_axis=0, tiled=True)
    restored = (returned[partner[0]].astype(jnp.float32) * scales[:, None, None]).reshape(
        row_count, columns
    )
    combined = jnp.where(live_mask, ladder + restored, jnp.zeros((), jnp.float32))
    two_body = combined.astype(jnp.bfloat16)[None]
    own_block = lax.dynamic_slice_in_dim(combined, blk_index * row_count, row_count, 1)
    weighted = jnp.diagonal(own_block) * degeneracy[0]
    orbit_match = orbital[0][:, None] == jnp.arange(NOB, dtype=jnp.int32)[None, :]
    partial_sums = jnp.sum(jnp.where(orbit_match, weighted[:, None], 0.0), axis=0)
    normalizer = 8.0 * math.sqrt(chan_count * columns / NOB)
    one_body = lax.psum(partial_sums, ("chan", "blk")) / normalizer
    return (two_body, one_body)


def widths_of(columns):
    unit = 256
    inner = columns - 2 * unit
    if inner <= 0 or inner % (2 * unit):
        return (unit,) * (columns // unit)
    return (unit,) + (2 * unit,) * (inner // (2 * unit)) + (unit,)


def fused_kernel(n, m, widths, scale, *refs):
    parts = len(widths)
    (
        gen_hbm,
        ham_hbm,
        pp_hbm,
        ph_hbm,
        partner_hbm,
        coupling_hbm,
        length_hbm,
        weight_hbm,
        orbital_hbm,
        out,
        sum_ref,
        pp_ref,
        ph_ref,
        partner_ref,
        coupling_ref,
        length_ref,
        weight_ref,
        orbital_ref,
        own_g,
        own_h,
        far_g,
        far_h,
        send_g,
        send_h,
        cross_g,
        cross_h,
        left,
        right,
        lad,
        diag,
        part,
        slots,
    ) = refs[:32]
    back = refs[32 : 32 + parts]
    ret = refs[32 + parts : 32 + 2 * parts]
    (
        small_sem,
        own_sem,
        x_send,
        x_recv,
        a_send,
        a_recv,
        r_send,
        r_recv,
        l_sem,
        b_send,
        b_recv,
        t_send,
        t_recv,
    ) = refs[32 + 2 * parts :]
    c = lax.axis_index("chan")
    b = lax.axis_index("blk")
    ob = 1 - b
    me = c * m + b
    count = n * m
    piece, columns = gen_hbm.shape[1:]
    rows = n * piece
    orbits = part.shape[1]
    twin = (c, ob)
    ends = [sum(widths[: j + 1]) for j in range(parts)]
    starts = [
        pl.multiple_of((1 - b) * (ends[j] - widths[j]) + b * (columns - ends[j]), 128)
        for j in range(parts)
    ]
    middle = [end >= rows for end in ends].index(True)
    raw = ((gen_hbm, own_g, far_g), (ham_hbm, own_h, far_h))
    sent = ((send_g, cross_g), (send_h, cross_h))
    small = (
        (pp_hbm, pp_ref),
        (ph_hbm, ph_ref),
        (partner_hbm, partner_ref),
        (coupling_hbm, coupling_ref),
        (length_hbm, length_ref),
        (weight_hbm, weight_ref),
        (orbital_hbm, orbital_ref),
    )

    def half_cols(half):
        return pl.ds(pl.multiple_of(half * rows, 128), rows)

    def slot(half, d):
        return pl.ds(pl.multiple_of((half * n + d) * piece, piece), piece)

    def strip(d):
        return pl.ds(pl.multiple_of(d * piece, piece), piece)

    level = n // 4
    z, y, x = c // level, c % level // 2, c % 2

    def chip(to, turn):
        return to * level + (y + turn // 2) % (level // 2) * 2 + (x + turn) % 2

    def pick(i, first, second, third):
        q, r = i // level, i % level
        own = q // 3
        to = first * ((1 - q) * (2 - q) // 2) + second * (q * (2 - q)) + third * (q * (q - 1) // 2)
        turn = r + b * (level - 1 - 2 * r)
        return chip(to * (1 - own) + z * own, turn * (1 - own) + (r + 1) * own)

    def target(i):
        return pick(i, 1 + z % 2, 3 * (1 - z % 2), (z + 2) % 4)

    def giver(i):
        return pick(i, 3 * (1 - z // 2), 2 - z // 2, z + 1 - 2 * (z % 2))

    def source(i):
        return pick(i, z + 1 - 2 * (z % 2), 2 - z // 2, 3 * (1 - z // 2))

    def each(count, body, first=0, unroll=1):
        def step(i, carry):
            body(i)
            return carry

        lax.fori_loop(first, count, step, 0, unroll=unroll)

    def small_copy(i):
        return pltpu.make_async_copy(small[i][0], small[i][1], small_sem.at[i])

    def own_copy(t):
        return pltpu.make_async_copy(raw[t][0], raw[t][1], own_sem.at[t])

    def twin_copy(t):
        return pltpu.make_async_remote_copy(
            src_ref=raw[t][0],
            dst_ref=raw[t][2],
            send_sem=x_send.at[t],
            recv_sem=x_recv.at[t],
            device_id=twin,
            device_id_type=MESH,
        )

    def piece_copy(t, k, d):
        return pltpu.make_async_remote_copy(
            src_ref=sent[t][0].at[strip(k)],
            dst_ref=sent[t][1].at[slot(b, d)],
            send_sem=a_send.at[t],
            recv_sem=a_recv.at[t, d],
            device_id=(k, b),
            device_id_type=MESH,
        )

    def relay(t, half, d):
        return pltpu.make_async_remote_copy(
            src_ref=sent[t][1].at[slot(half, d)],
            dst_ref=sent[t][1].at[slot(half, d)],
            send_sem=r_send.at[t],
            recv_sem=r_recv.at[t],
            device_id=twin,
            device_id_type=MESH,
        )

    def back_copy(j, k, d):
        return pltpu.make_async_remote_copy(
            src_ref=back[j].at[strip(k)],
            dst_ref=ret[j].at[d],
            send_sem=b_send.at[j],
            recv_sem=b_recv.at[j],
            device_id=(k, b),
            device_id_type=MESH,
        )

    others = pl.ds(0, (n - 1) * piece)

    def all_pieces(t):
        return pltpu.make_async_remote_copy(
            src_ref=sent[t][0].at[others],
            dst_ref=sent[t][1].at[others],
            send_sem=a_send.at[t],
            recv_sem=r_recv.at[t],
            device_id=twin,
            device_id_type=MESH,
        )

    def all_relays(t):
        where = pl.ds(pl.multiple_of(ob * rows, rows), rows)
        return pltpu.make_async_remote_copy(
            src_ref=sent[t][1].at[where],
            dst_ref=sent[t][1].at[where],
            send_sem=r_send.at[t],
            recv_sem=r_recv.at[t],
            device_id=twin,
            device_id_type=MESH,
        )

    def all_back(j):
        return pltpu.make_async_remote_copy(
            src_ref=back[j].at[others],
            dst_ref=ret[j].at[pl.ds(0, n - 1)],
            send_sem=b_send.at[j],
            recv_sem=b_recv.at[j],
            device_id=twin,
            device_id_type=MESH,
        )

    def back_local(j):
        return pltpu.make_async_copy(back[j].at[strip(c)], ret[j].at[c], l_sem.at[j])

    def peer(i):
        return (me + 1 + i) % count

    def total_copy(to, origin):
        return pltpu.make_async_remote_copy(
            src_ref=part,
            dst_ref=slots.at[origin],
            send_sem=t_send.at[to],
            recv_sem=t_recv.at[origin],
            device_id=(to // m, to % m),
            device_id_type=MESH,
        )

    for i in range(len(small)):
        small_copy(i).start()
    for t in range(2):
        own_copy(t).start()
    barrier = pltpu.get_barrier_semaphore()

    def greet(i):
        for core in range(m):
            pl.semaphore_signal(barrier, inc=1, device_id=(giver(i), core), device_id_type=MESH)

    each(n - 1, greet)
    pl.semaphore_signal(barrier, inc=1, device_id=twin, device_id_type=MESH)
    for i in range(len(small)):
        small_copy(i).wait()
    for t in range(2):
        own_copy(t).wait()
    length = length_ref[...]

    col_live = lax.broadcasted_iota(jnp.int32, (1, columns), 1) < length
    row_ids = lax.broadcasted_iota(jnp.int32, (piece, 1), 0)

    def prepare(k, refs_at):
        p, weight = jnp.int32(0), jnp.float32(0.0)
        for q in range(n):
            match = partner_ref[q] == k
            p = jnp.where(match, q, p)
            weight = jnp.where(match, coupling_ref[q], weight)
        factor = jnp.where(col_live, weight, 0.0)
        factor = jnp.where(row_ids + (b * n + p) * piece < length, factor, 0.0)
        for t in range(2):
            dst, where = refs_at[t]
            dst[where, :] = (raw[t][1][p].astype(jnp.float32) * factor).astype(jnp.bfloat16)

    def prepare_sent(i):
        k = target(i)
        prepare(k, [(send_g, strip(k)), (send_h, strip(k))])

    def send(i):
        k = target(i)
        for t in range(2):
            piece_copy(t, k, c).start()

    ahead = 2
    each(ahead, prepare_sent)
    pl.semaphore_wait(barrier, count - 1)
    distant = n - level

    def send_and_prepare(i):
        send(i)
        prepare_sent(i + ahead)

    each(distant - ahead, send_and_prepare)
    each(distant, send, distant - ahead)
    prepare(c, [(cross_g, slot(b, c)), (cross_h, slot(b, c))])
    for t in range(2):
        twin_copy(t).start()
    each(n - 1, prepare_sent, distant)

    def pp_scale(i):
        factor = jnp.where(col_live, pp_ref[...], 0.0)
        left[strip(i), :] = (own_g[i].astype(jnp.float32) * factor).astype(jnp.bfloat16)
        right[strip(i), :] = (own_h[i].astype(jnp.float32) * factor).astype(jnp.bfloat16)

    each(n, pp_scale)

    def dot(x, y):
        return jnp.dot(x, y, preferred_element_type=jnp.float32)

    for t in range(2):
        relay(t, b, c).start()
        twin_copy(t).wait_recv()
    unit = 256

    def ladder_step(j):
        cols = pl.ds(pl.multiple_of(j * unit, unit), unit)
        near, other = half_cols(b), half_cols(ob)
        lad[:, cols] = (
            dot(left[:, near], own_h[:, :, cols].reshape(rows, unit))
            + dot(left[:, other], far_h[:, :, cols].reshape(rows, unit))
            - dot(right[:, near], own_g[:, :, cols].reshape(rows, unit))
            - dot(right[:, other], far_g[:, :, cols].reshape(rows, unit))
        )

    each(columns // unit, ladder_step)
    each(n - 1, send, distant)

    def ph_scale(d):
        factor = ph_ref[...]
        left[strip(d), :] = (cross_g[slot(b, d), :].astype(jnp.float32) * factor).astype(jnp.bfloat16)
        right[strip(d), :] = (cross_h[slot(b, d), :].astype(jnp.float32) * factor).astype(jnp.bfloat16)

    ph_scale(c)

    def take(i):
        d = source(i)
        for t in range(2):
            piece_copy(t, d, d).wait_recv()
            relay(t, b, d).start()
        ph_scale(d)

    each(n - 1, take)

    for t in range(2):
        all_relays(t).wait_recv()

    def give(j):
        def step(i):
            back_copy(j, giver(i), c).start()

        each(n - 1, step)
        back_local(j).start()

    for j in range(parts):
        cols = pl.ds(starts[j], widths[j])
        back[j][...] = (dot(left[...], cross_h[:, cols]) - dot(right[...], cross_g[:, cols])).astype(
            jnp.bfloat16
        )

        if j <= middle + 1:
            give(j)

    for t in range(2):
        twin_copy(t).wait_send()
        all_pieces(t).wait_send()
        all_relays(t).wait_send()

    def total_take(i):
        other = peer(i)
        total_copy(other, me).wait_send()
        total_copy(other, other).wait_recv()

    first = b * rows
    for j in range(parts):
        if j + 1 == parts:
            each(count - 1, total_take)
            sum_ref[...] = jnp.sum(slots[...], axis=0) * scale
            for i in range(j):
                all_back(i).wait_send()
        all_back(j).wait_recv()
        back_local(j).wait()
        cols = pl.ds(starts[j], widths[j])
        col_ids = starts[j] + lax.broadcasted_iota(jnp.int32, (1, widths[j]), 1)
        if j <= middle:
            diag[:, cols] = jnp.zeros((1, widths[j]), jnp.float32)

        def fold(p, j=j, cols=cols, col_ids=col_ids):
            ids = row_ids + (first + p * piece)
            value = lad[strip(p), cols] + ret[j][partner_ref[p]].astype(jnp.float32) * coupling_ref[p]
            value = jnp.where((ids < length) & (col_ids < length), value, 0.0)
            out[strip(p), cols] = value.astype(jnp.bfloat16)
            if j <= middle:
                diag[:, cols] += jnp.sum(jnp.where(ids == col_ids, value, 0.0), axis=0, keepdims=True)

        each(n, fold, unroll=4)
        if j != middle:
            continue
        weighted = diag[:, half_cols(b)] * weight_ref[...]
        hits = lax.broadcasted_iota(jnp.int32, (orbits, rows), 0) == orbital_ref[...]
        part[...] = lax.dot_general(
            weighted,
            jnp.where(hits, 1.0, 0.0),
            (((1,), (1,)), ((), ())),
            precision=lax.Precision.HIGHEST,
            preferred_element_type=jnp.float32,
        )

        def total_send(i):
            total_copy(peer(i), me).start()

        each(count - 1, total_send)
        for i in range(middle + 2, parts):
            give(i)
        slots[me] = part[...]

    all_back(parts - 1).wait_send()


def on_device(
    generator,
    hamiltonian,
    pp_occupancy,
    ph_occupancy,
    lengths,
    partner,
    coupling,
    degeneracy,
    orbital,
):
    n = lax.axis_size("chan")
    m = lax.axis_size("blk")
    rows, columns = generator.shape[1:]
    widths = widths_of(columns)
    parts = len(widths)
    orbits = -(-NOB // 128) * 128
    anywhere = pl.BlockSpec(memory_space=pl.ANY)
    hbm = pl.BlockSpec(memory_space=pltpu.HBM)
    vmem = pl.BlockSpec(memory_space=pltpu.VMEM)
    dma = pltpu.SemaphoreType.DMA
    half = pltpu.VMEM((rows, columns), jnp.bfloat16)
    full = pltpu.VMEM((2 * rows, columns), jnp.bfloat16)
    cut = pltpu.VMEM((n, rows // n, columns), jnp.bfloat16)
    strips = [pltpu.VMEM((rows, w), jnp.bfloat16) for w in widths]
    cuts = [pltpu.VMEM((n, rows // n, w), jnp.bfloat16) for w in widths]
    scale = 1.0 / (8.0 * math.sqrt(n * columns / NOB))
    two_body, sums = pl.pallas_call(
        functools.partial(fused_kernel, n, m, widths, scale),
        out_shape=(
            pltpu.VMEM((rows, columns), jnp.bfloat16),
            pltpu.VMEM((1, orbits), jnp.float32),
        ),
        in_specs=[anywhere] * 2 + [hbm] * 7,
        out_specs=(vmem, vmem),
        scratch_shapes=[
            pltpu.VMEM((1, columns), jnp.float32),
            pltpu.VMEM((1, columns), jnp.float32),
            pltpu.SMEM((n,), jnp.int32),
            pltpu.SMEM((n,), jnp.float32),
            pltpu.VMEM((1, 1), jnp.int32),
            pltpu.VMEM((1, 1), jnp.float32),
            pltpu.VMEM((1, rows), jnp.int32),
        ]
        + [cut] * 4
        + [half] * 2
        + [full] * 2
        + [half] * 2
        + [
            pltpu.VMEM((rows, columns), jnp.float32),
            pltpu.VMEM((1, columns), jnp.float32),
            pltpu.VMEM((1, orbits), jnp.float32),
            pltpu.VMEM((n * m, 1, orbits), jnp.float32),
        ]
        + strips
        + cuts
        + [
            dma((7,)),
            dma((2,)),
            dma((2,)),
            dma((2,)),
            dma((2,)),
            dma((2, n)),
            dma((2,)),
            dma((2,)),
            dma((parts,)),
            dma((parts,)),
            dma((parts,)),
            dma((n * m,)),
            dma((n * m,)),
        ],
        compiler_params=pltpu.CompilerParams(
            collective_id=0, has_side_effects=True, vmem_limit_bytes=VMEM_LIMIT
        ),
        name="fused",
    )(
        generator.reshape(n, rows // n, columns),
        hamiltonian.reshape(n, rows // n, columns),
        pp_occupancy,
        ph_occupancy,
        partner[0],
        coupling[0],
        lengths[None],
        degeneracy[None],
        orbital,
    )
    return (two_body[None], sums[0, :NOB])


def solution(mesh):
    placed = (
        P("chan", "blk", None),
        P("chan", "blk", None),
        P("chan", None),
        P("chan", None),
        P("chan"),
        P("chan", None),
        P("chan", None),
        P("chan"),
        P("chan", "blk"),
    )
    n, m = mesh.shape["chan"], mesh.shape["blk"]

    def body(*args):
        rows, columns = args[0].shape[1:]
        tiled = m == 2 and n % 8 == 0 and rows % (16 * n) == 0 and columns % 256 == 0
        return (on_device if tiled else on_device_plain)(*args)

    return jax.shard_map(
        body,
        mesh=mesh,
        in_specs=placed,
        out_specs=(P("chan", "blk", None), P()),
        check_vma=False,
    )
```
